32 devices in a mesh: seqa: 4 (over x, core), seqb: 8 (over z, y).
Axes of the slice: x: 2, y: 2, z: 4, core: 2. Of those that a mesh axis runs over, the one named last changes fastest.
Arguments:
- sequence_input: bfloat16 [16384, 640], P(('seqa', 'seqb')), may hold values from -6 to 6
- w_prev: bfloat16 [3, 640, 1280], P(None, 'seqa'), may hold values from -0.15625 to 0.15625
- w_now: bfloat16 [3, 640, 1280], P(None, 'seqa'), may hold values from -0.15625 to 0.15625
- conv_bias: float32 [3, 1280], replicated, may hold values from -4 to 4
- w_mix: bfloat16 [3, 640, 640], P(None, None, 'seqa'), may hold values from -0.25 to 0.25
Outputs:
- seq_out: bfloat16 [16384, 640], P(('seqa', 'seqb'))
The draws below stay inside these ranges and needn't reach their ends.
All inputs are finite; a program needn't handle non-finite values.
Results may differ from the reference program's by a relative error of at most 0.0052.
Values may be sent and summed in bfloat16 or wider, within the bound.
A program may use at most 64 MiB of HBM per device.

```python
import jax
import jax.numpy as jnp
from jax import lax

D = 640
LAYERS = 3
DILATION_FIRST1 = 128
DILATION_SECOND2 = 512
DILATION_THIRD3 = 2048
TOTAL = 16384


def shard_levels(key, extent, shards, low, largest):
    level, own = 1.0, jax.random.fold_in(key, 6)
    for axis_at, blocks in shards:
        draws = jnp.exp(jax.random.uniform(jax.random.fold_in(own, axis_at), (blocks,), jnp.float32, low / len(shards), largest / len(shards)))
        level = level * jnp.repeat(draws, extent[axis_at] // blocks).reshape([-1 if axis == axis_at else 1 for axis in range(len(extent))])
    return level


def gaussian(rng, shape, width, most, cuts=(), held_as=jnp.bfloat16):
    factor_of = shard_levels(rng, shape, cuts, -0.22, 0.18) if cuts else 1.0
    array = jax.random.normal(rng, shape, jnp.float32) * width * factor_of
    return jnp.minimum(jnp.maximum(array, -most), most).astype(held_as)


def setup_inputs(seed: int = 0) -> dict:
    arg_keys = jax.random.split(jax.random.key(seed), 6)
    sequence_input = gaussian(arg_keys[0], (TOTAL, D), 1.0, 6.0, ((0, 32),))
    w_prev = gaussian(arg_keys[1], (LAYERS, D, 2 * D), (2 * D) ** -0.5, 0.15625, ((1, 4),))
    w_now = gaussian(arg_keys[2], (LAYERS, D, 2 * D), (2 * D) ** -0.5, 0.15625, ((1, 4),))
    conv_bias = gaussian(arg_keys[3], (LAYERS, 2 * D), 1.0, 4.0, (), jnp.float32)
    w_mix = gaussian(arg_keys[4], (LAYERS, D, D), D ** -0.5, 0.25, ((2, 4),))
    return dict(sequence_input=sequence_input, w_prev=w_prev, w_now=w_now, conv_bias=conv_bias, w_mix=w_mix)


def norm_rows(values):
    scale = lax.rsqrt(lax.optimization_barrier(jnp.mean(values * values, axis=1, keepdims=True)) + 1e-06)
    return (values * scale).astype(jnp.bfloat16)

def reference(sequence_input, w_prev, w_now, conv_bias, w_mix):
    hidden_state = sequence_input.astype(jnp.float32)
    for layer_index, dilation_step in enumerate((DILATION_FIRST1, DILATION_SECOND2, DILATION_THIRD3)):
        normed = norm_rows(hidden_state)
        earlier = jnp.pad(normed, ((dilation_step, 0), (0, 0)))[:normed.shape[0]]
        pre = jnp.dot(earlier, w_prev[layer_index], preferred_element_type=jnp.float32)
        pre = pre + jnp.dot(normed, w_now[layer_index], preferred_element_type=jnp.float32)
        pre = pre + conv_bias[layer_index]
        hidden = (pre[:, :D] * jax.nn.sigmoid(pre[:, D:])).astype(jnp.bfloat16)
        hidden_state = hidden_state + jnp.dot(hidden, w_mix[layer_index], preferred_element_type=jnp.float32)
    return hidden_state.astype(jnp.bfloat16)
```

```python
import functools

import jax
import jax.numpy as jnp
from jax import lax
from jax.experimental import pallas as pl
from jax.experimental.pallas import tpu as pltpu
from jax.sharding import PartitionSpec as P

DILATIONS = (128, 512, 2048)
EPS = 1e-06
TILE = 16
GROUP = 4
MESH_ID = pl.DeviceIdType.MESH


def from_behind(value, axis, by):
    peers = lax.axis_size(axis)
    pairs = [(i, i + by) for i in range(peers) if 0 <= i + by < peers]
    return lax.ppermute(value, axis, pairs)


def norm_rows(values):
    scale = lax.rsqrt(jnp.mean(values * values, axis=1, keepdims=True) + EPS)
    return (values * scale).astype(jnp.bfloat16)


def block_prior(normed, dilation_step):
    rows = normed.shape[0]
    whole = dilation_step // rows
    part = dilation_step % rows
    pieces = []
    if part > 0:
        pieces.append(from_behind(normed[rows - part :], ("seqa", "seqb"), whole + 1))
    head = normed[: rows - part]
    if whole > 0:
        head = from_behind(head, ("seqa", "seqb"), whole)
    pieces.append(head)
    return jnp.concatenate(pieces, axis=0)


def one_layer(hidden_state, tap_prev, tap_now, bias, mixing, dilation_step):
    normed = norm_rows(hidden_state)
    earlier = block_prior(normed, dilation_step)
    dim = hidden_state.shape[1]
    pre = bias[None, :] + jnp.dot(
        earlier,
        lax.all_gather(tap_prev, "seqa", axis=0, tiled=True),
        preferred_element_type=jnp.float32,
    )
    pre = pre + jnp.dot(
        normed,
        lax.all_gather(tap_now, "seqa", axis=0, tiled=True),
        preferred_element_type=jnp.float32,
    )
    hidden = (pre[:, :dim] * jax.nn.sigmoid(pre[:, dim:])).astype(jnp.bfloat16)
    return hidden_state + jnp.dot(
        hidden,
        lax.all_gather(mixing, "seqa", axis=1, tiled=True),
        preferred_element_type=jnp.float32,
    )


def plain_local(sequence_input, w_prev, w_now, conv_bias, w_mix):
    state = sequence_input.astype(jnp.float32)
    for layer, step in enumerate(DILATIONS):
        state = one_layer(
            state, w_prev[layer], w_now[layer], conv_bias[layer], w_mix[layer], step
        )
    return state.astype(jnp.bfloat16)


def flip(value, bit):
    return value + bit - 2 * bit * ((value // bit) % 2)


def block_kernel(
    na, nb, chunk,
    x_hbm, wp_hbm, wn_hbm, bias_ref, wm_hbm,
    out_ref,
    w, xin, tail, state, u0, u1, u2, h1, h2, pre,
    load_sem, x_sem, send, recv, halo_send, halo_recv,
):
    layers, dim = wp_hbm.shape[0], x_hbm.shape[1]
    wide = 2 * dim
    shard = wp_hbm.shape[1]
    rows = x_hbm.shape[0]
    n = na * nb
    part = DILATIONS[0]
    chunks = rows // chunk
    a, b = lax.axis_index("seqa"), lax.axis_index("seqb")
    me = a * nb + b
    a1, a2 = flip(a, 1), flip(a, 2)
    b1, b2 = flip(b, 1), flip(b, 2)
    p = b % GROUP
    p1, p2 = flip(p, 1), flip(p, 2)
    p3 = flip(p1, 2)
    big = 2 * TILE
    direct = GROUP * big

    def at(index):
        return (index // nb, index % nb)

    hops = (1, DILATIONS[1] // rows, DILATIONS[2] // rows)

    loads = []
    for l in range(layers):
        loads.append([
            pltpu.make_async_copy(wp_hbm.at[l], w.at[l, a, :, pl.ds(0, wide)], load_sem.at[l, 0]),
            pltpu.make_async_copy(wn_hbm.at[l], w.at[l, a, :, pl.ds(wide, wide)], load_sem.at[l, 1]),
            pltpu.make_async_copy(wm_hbm.at[l], w.at[l, a, :, pl.ds(2 * wide, dim)], load_sem.at[l, 2]),
        ])
    for c in loads[0]:
        c.start()
    x_load = pltpu.make_async_copy(x_hbm, xin, x_sem)
    x_load.start()
    for l in range(1, layers):
        for c in loads[l]:
            c.start()

    barrier = pltpu.get_barrier_semaphore()
    near = [(a1, b), (a2, b), (a, b1), (a, b2)]
    for h in sorted(set(hops)):
        near += [at((me + h) % n), at((me + n - h) % n)]
    for dev in near:
        pl.semaphore_signal(barrier, inc=1, device_id=dev, device_id_type=MESH_ID)
    pl.semaphore_wait(barrier, len(near))

    def move(l, k, owner, start, size, dev):
        ref = w.at[l, owner, pl.ds(pl.multiple_of(start, TILE), size)]
        return pltpu.make_async_remote_copy(
            src_ref=ref, dst_ref=ref, send_sem=send.at[l, k], recv_sem=recv.at[l, k],
            device_id=dev, device_id_type=MESH_ID,
        )

    core, across, ynear, znear = (a1, b), (a2, b), (a, b1), (a, b2)
    moves = []
    for l in range(layers):
        moves.append([
            move(l, 0, a, p * big, big, across),
            move(l, 1, a, direct, shard - direct, across),
            move(l, 2, a, 0, shard, core),
            move(l, 3, a2, p * big, big, ynear),
            move(l, 4, a2, p * big, big, znear),
            move(l, 5, a2, p * big, big, core),
            move(l, 6, a2, direct, shard - direct, core),
            move(l, 7, a2, p1 * big, TILE, znear),
            move(l, 8, a2, p1 * big, big, core),
            move(l, 9, a2, p2 * big + TILE, TILE, ynear),
            move(l, 10, a2, p2 * big, big, core),
            move(l, 11, a2, p3 * big, TILE, core),
            move(l, 12, a2, p3 * big + TILE, TILE, core),
        ])

    def after(l, k, then):
        moves[l][k].wait_recv()
        for t in then:
            moves[l][t].start()

    def forward_first(l):
        after(l, 0, (3, 4, 5))

    def forward_rest(l):
        after(l, 3, (7, 8))
        after(l, 4, (9, 10))
        after(l, 1, (6,))
        after(l, 7, (11,))
        after(l, 9, (12,))

    def finish(l):
        for k in (2, 5, 6, 8, 10, 11, 12):
            after(l, k, ())

    def halo(slot, src, dst, hop):
        return pltpu.make_async_remote_copy(
            src_ref=src, dst_ref=dst, send_sem=halo_send.at[slot], recv_sem=halo_recv.at[slot],
            device_id=at((me + hop) % n), device_id_type=MESH_ID,
        )

    tail_copy = halo(0, xin.at[pl.ds(rows - part, part)], tail, 1)
    h1_copies = [
        halo(1 + c, u1.at[pl.ds(c * chunk, chunk)], h1.at[pl.ds(c * chunk, chunk)], hops[1])
        for c in range(chunks)
    ]
    h2_copies = [
        halo(1 + chunks + c, u2.at[pl.ds(c * chunk, chunk)], h2.at[pl.ds(c * chunk, chunk)], hops[2])
        for c in range(chunks)
    ]
    copies = [(tail_copy, 1)] + [(c, hops[1]) for c in h1_copies] + [(c, hops[2]) for c in h2_copies]

    def send_halo(copy, hop):
        @pl.when(me + hop < n)
        def _():
            copy.start()

    def take_halo(copy, hop):
        @pl.when(me >= hop)
        def _():
            copy.wait_recv()

    for l in range(layers):
        for c in loads[l]:
            c.wait()
        if l == 0:
            moves[l][0].start()
            moves[l][1].start()
            moves[l][2].start()
            x_load.wait()
            send_halo(tail_copy, hops[0])
        elif l == 1:
            moves[l][0].start()
            moves[l][1].start()
            moves[l][2].start()
        else:
            moves[l][2].start()

    @pl.when(me < hops[0])
    def _():
        tail[...] = jnp.zeros_like(tail)

    @pl.when(me < hops[1])
    def _():
        h1[...] = jnp.zeros_like(h1)

    @pl.when(me < hops[2])
    def _():
        h2[...] = jnp.zeros_like(h2)

    first = xin[...].astype(jnp.float32)
    state[...] = first
    u0[pl.ds(part, rows), :] = norm_rows(first)

    forward_first(0)
    take_halo(tail_copy, hops[0])
    u0[pl.ds(0, part), :] = norm_rows(tail[...].astype(jnp.float32))
    forward_rest(0)
    finish(0)

    def tap(l, lo):
        return w[l, :, :, lo : lo + wide].reshape(na * shard, wide)

    def now_part(l, u, lo, r0):
        pre[pl.ds(r0, chunk), :] = bias_ref[l : l + 1, :] + jnp.dot(
            u[pl.ds(lo, chunk), :], tap(l, wide), preferred_element_type=jnp.float32
        )

    def rest_part(l, earlier, r0):
        total = pre[pl.ds(r0, chunk), :] + jnp.dot(
            earlier[pl.ds(r0, chunk), :], tap(l, 0), preferred_element_type=jnp.float32
        )
        hidden = (total[:, :dim] * jax.nn.sigmoid(total[:, dim:])).astype(jnp.bfloat16)
        mix = w[l, :, :, 2 * wide :].reshape(na * shard, dim)
        return state[pl.ds(r0, chunk), :] + lax.dot_general(
            hidden, mix, (((1,), (1,)), ((), ())), preferred_element_type=jnp.float32
        )

    for c in range(chunks):
        r0 = c * chunk
        now_part(0, u0, part + r0, r0)
        new = rest_part(0, u0, r0)
        state[pl.ds(r0, chunk), :] = new
        u1[pl.ds(r0, chunk), :] = norm_rows(new)
        if c == 0:
            forward_first(1)
        send_halo(h1_copies[c], hops[1])
    moves[2][0].start()
    moves[2][1].start()
    forward_rest(1)
    finish(1)
    for c in range(chunks):
        now_part(1, u1, c * chunk, c * chunk)
    for c in range(chunks):
        r0 = c * chunk
        take_halo(h1_copies[c], hops[1])
        new = rest_part(1, h1, r0)
        state[pl.ds(r0, chunk), :] = new
        u2[pl.ds(r0, chunk), :] = norm_rows(new)
        if c == 0:
            forward_first(2)
        send_halo(h2_copies[c], hops[2])
    forward_rest(2)
    finish(2)
    for c in range(chunks):
        now_part(2, u2, c * chunk, c * chunk)
    for c in range(chunks):
        r0 = c * chunk
        take_halo(h2_copies[c], hops[2])
        out_ref[pl.ds(r0, chunk), :] = rest_part(2, h2, r0).astype(out_ref.dtype)

    for l in range(layers):
        for m in moves[l]:
            m.wait_send()
    for copy, hop in copies:
        @pl.when(me + hop < n)
        def _(copy=copy):
            copy.wait_send()


def kernel_local(na, nb, sequence_input, w_prev, w_now, conv_bias, w_mix):
    rows, dim = sequence_input.shape
    layers, shard, wide = w_prev.shape
    chunk = rows // 2
    part = DILATIONS[0]
    bf16, f32 = jnp.bfloat16, jnp.float32
    halos = 1 + 2 * (rows // chunk)
    anywhere = pl.BlockSpec(memory_space=pl.ANY)
    vmem = pl.BlockSpec(memory_space=pltpu.VMEM)
    return pl.pallas_call(
        functools.partial(block_kernel, na, nb, chunk),
        out_shape=jax.ShapeDtypeStruct((rows, dim), bf16),
        in_specs=[anywhere, anywhere, anywhere, vmem, anywhere],
        out_specs=vmem,
        scratch_shapes=[
            pltpu.VMEM((layers, na, shard, 2 * wide + dim), bf16),
            pltpu.VMEM((rows, dim), bf16),
            pltpu.VMEM((part, dim), bf16),
            pltpu.VMEM((rows, dim), f32),
            pltpu.VMEM((part + rows, dim), bf16),
            pltpu.VMEM((rows, dim), bf16),
            pltpu.VMEM((rows, dim), bf16),
            pltpu.VMEM((rows, dim), bf16),
            pltpu.VMEM((rows, dim), bf16),
            pltpu.VMEM((rows, wide), f32),
            pltpu.SemaphoreType.DMA((layers, 3)),
            pltpu.SemaphoreType.DMA,
            pltpu.SemaphoreType.DMA((layers, 13)),
            pltpu.SemaphoreType.DMA((layers, 13)),
            pltpu.SemaphoreType.DMA((halos,)),
            pltpu.SemaphoreType.DMA((halos,)),
        ],
        compiler_params=pltpu.CompilerParams(
            collective_id=0, has_side_effects=True, vmem_limit_bytes=56 * 2**20
        ),
    )(sequence_input, w_prev, w_now, conv_bias, jnp.swapaxes(w_mix, 1, 2))


def local(na, nb, sequence_input, w_prev, w_now, conv_bias, w_mix):
    rows = sequence_input.shape[0]
    shard = w_prev.shape[1]
    fits = (
        na == 4
        and nb % GROUP == 0
        and shard % TILE == 0
        and shard > GROUP * 2 * TILE
        and rows % (4 * TILE) == 0
        and DILATIONS[0] < rows
        and DILATIONS[1] % rows == 0
        and DILATIONS[2] % rows == 0
    )
    body = functools.partial(kernel_local, na, nb) if fits else plain_local
    return body(sequence_input, w_prev, w_now, conv_bias, w_mix)


def solution(mesh):
    return jax.shard_map(
        functools.partial(local, mesh.shape["seqa"], mesh.shape["seqb"]),
        mesh=mesh,
        in_specs=(
            P(("seqa", "seqb"), None),
            P(None, "seqa", None),
            P(None, "seqa", None),
            P(),
            P(None, None, "seqa"),
        ),
        out_specs=P(("seqa", "seqb"), None),
        check_vma=False,
    )
```

```python
import functools

import jax
import jax.numpy as jnp
from jax import lax
from jax.experimental import pallas as pl
from jax.experimental.pallas import tpu as pltpu
from jax.sharding import PartitionSpec as P

DILATIONS = (128, 512, 2048)
EPS = 1e-06
TILE = 16
GROUP = 4
MESH_ID = pl.DeviceIdType.MESH


def from_behind(value, axis, by):
    peers = lax.axis_size(axis)
    pairs = [(i, i + by) for i in range(peers) if 0 <= i + by < peers]
    return lax.ppermute(value, axis, pairs)


def norm_rows(values):
    scale = lax.rsqrt(jnp.mean(values * values, axis=1, keepdims=True) + EPS)
    return (values * scale).astype(jnp.bfloat16)


def block_prior(normed, dilation_step):
    rows = normed.shape[0]
    whole = dilation_step // rows
    part = dilation_step % rows
    pieces = []
    if part > 0:
        pieces.append(from_behind(normed[rows - part :], ("seqa", "seqb"), whole + 1))
    head = normed[: rows - part]
    if whole > 0:
        head = from_behind(head, ("seqa", "seqb"), whole)
    pieces.append(head)
    return jnp.concatenate(pieces, axis=0)


def one_layer(hidden_state, tap_prev, tap_now, bias, mixing, dilation_step):
    normed = norm_rows(hidden_state)
    earlier = block_prior(normed, dilation_step)
    dim = hidden_state.shape[1]
    pre = bias[None, :] + jnp.dot(
        earlier,
        lax.all_gather(tap_prev, "seqa", axis=0, tiled=True),
        preferred_element_type=jnp.float32,
    )
    pre = pre + jnp.dot(
        normed,
        lax.all_gather(tap_now, "seqa", axis=0, tiled=True),
        preferred_element_type=jnp.float32,
    )
    hidden = (pre[:, :dim] * jax.nn.sigmoid(pre[:, dim:])).astype(jnp.bfloat16)
    return hidden_state + jnp.dot(
        hidden,
        lax.all_gather(mixing, "seqa", axis=1, tiled=True),
        preferred_element_type=jnp.float32,
    )


def plain_local(sequence_input, w_prev, w_now, conv_bias, w_mix):
    state = sequence_input.astype(jnp.float32)
    for layer, step in enumerate(DILATIONS):
        state = one_layer(
            state, w_prev[layer], w_now[layer], conv_bias[layer], w_mix[layer], step
        )
    return state.astype(jnp.bfloat16)


def flip(value, bit):
    return value + bit - 2 * bit * ((value // bit) % 2)


def block_kernel(
    na, nb, chunk,
    x_hbm, wp_hbm, wn_hbm, bias_ref, wm_hbm,
    out_ref,
    w, xin, tail, state, u0, u1, u2, h1, h2, pre,
    load_sem, x_sem, send, recv, halo_send, halo_recv,
):
    layers, dim = wp_hbm.shape[0], x_hbm.shape[1]
    wide = 2 * dim
    shard = wp_hbm.shape[1]
    rows = x_hbm.shape[0]
    n = na * nb
    part = DILATIONS[0]
    chunks = rows // chunk
    a, b = lax.axis_index("seqa"), lax.axis_index("seqb")
    me = a * nb + b
    a1, a2 = flip(a, 1), flip(a, 2)
    b1, b2 = flip(b, 1), flip(b, 2)
    p = b % GROUP
    p1, p2 = flip(p, 1), flip(p, 2)
    p3 = flip(p1, 2)
    big = 2 * TILE
    direct = GROUP * big

    def at(index):
        return (index // nb, index % nb)

    hops = (1, DILATIONS[1] // rows, DILATIONS[2] // rows)

    loads = []
    for l in range(layers):
        loads.append([
            pltpu.make_async_copy(wp_hbm.at[l], w.at[l, a, :, pl.ds(0, wide)], load_sem.at[l, 0]),
            pltpu.make_async_copy(wn_hbm.at[l], w.at[l, a, :, pl.ds(wide, wide)], load_sem.at[l, 1]),
            pltpu.make_async_copy(wm_hbm.at[l], w.at[l, a, :, pl.ds(2 * wide, dim)], load_sem.at[l, 2]),
        ])
    for c in loads[0]:
        c.start()
    x_load = pltpu.make_async_copy(x_hbm, xin, x_sem)
    x_load.start()
    for l in range(1, layers):
        for c in loads[l]:
            c.start()

    barrier = pltpu.get_barrier_semaphore()
    near = [(a1, b), (a2, b), (a, b1), (a, b2)]
    for h in sorted(set(hops)):
        near += [at((me + h) % n), at((me + n - h) % n)]
    for dev in near:
        pl.semaphore_signal(barrier, inc=1, device_id=dev, device_id_type=MESH_ID)
    pl.semaphore_wait(barrier, len(near))

    def move(l, k, owner, start, size, dev):
        ref = w.at[l, owner, pl.ds(pl.multiple_of(start, TILE), size)]
        return pltpu.make_async_remote_copy(
            src_ref=ref, dst_ref=ref, send_sem=send.at[l, k], recv_sem=recv.at[l, k],
            device_id=dev, device_id_type=MESH_ID,
        )

    core, across, ynear, znear = (a1, b), (a2, b), (a, b1), (a, b2)
    moves = []
    for l in range(layers):
        moves.append([
            move(l, 0, a, p * big, TILE, across),
            move(l, 1, a, p * big + TILE, TILE, across),
            move(l, 2, a, direct, shard - direct, across),
            move(l, 3, a, 0, shard, core),
            move(l, 4, a2, p * big, TILE, ynear),
            move(l, 5, a2, p * big, TILE, znear),
            move(l, 6, a2, p * big + TILE, TILE, ynear),
            move(l, 7, a2, p * big + TILE, TILE, znear),
            move(l, 8, a2, p * big, big, core),
            move(l, 9, a2, direct, shard - direct, core),
            move(l, 10, a2, p1 * big, TILE, znear),
            move(l, 11, a2, p1 * big, big, core),
            move(l, 12, a2, p2 * big + TILE, TILE, ynear),
            move(l, 13, a2, p2 * big, big, core),
            move(l, 14, a2, p3 * big, TILE, core),
            move(l, 15, a2, p3 * big + TILE, TILE, core),
        ])

    def after(l, k, then):
        moves[l][k].wait_recv()
        for t in then:
            moves[l][t].start()

    def forward_first(l):
        after(l, 0, (4, 5))
        after(l, 1, (6, 7, 8))

    def forward_second(l):
        after(l, 4, (10,))
        after(l, 5, ())
        after(l, 7, (12, 13))
        after(l, 6, (11,))

    def forward_last(l):
        after(l, 10, (14,))
        after(l, 12, (15,))

    def forward_direct(l):
        after(l, 2, (9,))

    def finish(l):
        for k in (3, 8, 9, 11, 13, 14, 15):
            after(l, k, ())

    def halo(slot, src, dst, hop):
        return pltpu.make_async_remote_copy(
            src_ref=src, dst_ref=dst, send_sem=halo_send.at[slot], recv_sem=halo_recv.at[slot],
            device_id=at((me + hop) % n), device_id_type=MESH_ID,
        )

    tail_copy = halo(0, xin.at[pl.ds(rows - part, part)], tail, 1)
    h1_copies = [
        halo(1 + c, u1.at[pl.ds(c * chunk, chunk)], h1.at[pl.ds(c * chunk, chunk)], hops[1])
        for c in range(chunks)
    ]
    h2_copies = [
        halo(1 + chunks + c, u2.at[pl.ds(c * chunk, chunk)], h2.at[pl.ds(c * chunk, chunk)], hops[2])
        for c in range(chunks)
    ]
    copies = [(tail_copy, 1)] + [(c, hops[1]) for c in h1_copies] + [(c, hops[2]) for c in h2_copies]

    def send_halo(copy, hop):
        @pl.when(me + hop < n)
        def _():
            copy.start()

    def take_halo(copy, hop):
        @pl.when(me >= hop)
        def _():
            copy.wait_recv()

    for c in loads[0]:
        c.wait()
    moves[0][0].start()
    moves[0][1].start()
    x_load.wait()
    send_halo(tail_copy, hops[0])
    for c in loads[1]:
        c.wait()
    moves[1][0].start()
    moves[1][1].start()
    moves[0][2].start()
    moves[0][3].start()
    for c in loads[2]:
        c.wait()
    moves[1][2].start()
    moves[1][3].start()
    for k in (0, 1, 2, 3):
        moves[2][k].start()

    @pl.when(me < hops[0])
    def _():
        tail[...] = jnp.zeros_like(tail)

    @pl.when(me < hops[1])
    def _():
        h1[...] = jnp.zeros_like(h1)

    @pl.when(me < hops[2])
    def _():
        h2[...] = jnp.zeros_like(h2)

    first = xin[...].astype(jnp.float32)
    state[...] = first
    u0[pl.ds(part, rows), :] = norm_rows(first)

    forward_first(0)
    take_halo(tail_copy, hops[0])
    u0[pl.ds(0, part), :] = norm_rows(tail[...].astype(jnp.float32))
    forward_second(0)
    forward_first(1)
    forward_last(0)
    forward_direct(0)
    finish(0)

    def tap(l, lo):
        return w[l, :, :, lo : lo + wide].reshape(na * shard, wide)

    def now_part(l, u, lo, r0):
        pre[pl.ds(r0, chunk), :] = bias_ref[l : l + 1, :] + jnp.dot(
            u[pl.ds(lo, chunk), :], tap(l, wide), preferred_element_type=jnp.float32
        )

    def rest_part(l, earlier, r0):
        total = pre[pl.ds(r0, chunk), :] + jnp.dot(
            earlier[pl.ds(r0, chunk), :], tap(l, 0), preferred_element_type=jnp.float32
        )
        hidden = (total[:, :dim] * jax.nn.sigmoid(total[:, dim:])).astype(jnp.bfloat16)
        mix = w[l, :, :, 2 * wide :].reshape(na * shard, dim)
        return state[pl.ds(r0, chunk), :] + lax.dot_general(
            hidden, mix, (((1,), (1,)), ((), ())), preferred_element_type=jnp.float32
        )

    for c in range(chunks):
        r0 = c * chunk
        now_part(0, u0, part + r0, r0)
        if c == 0:
            forward_second(1)
        new = rest_part(0, u0, r0)
        state[pl.ds(r0, chunk), :] = new
        u1[pl.ds(r0, chunk), :] = norm_rows(new)
        send_halo(h1_copies[c], hops[1])
        if c == 0:
            forward_last(1)
    forward_direct(1)
    finish(1)
    for c in range(chunks):
        now_part(1, u1, c * chunk, c * chunk)
    forward_first(2)
    for c in range(chunks):
        r0 = c * chunk
        take_halo(h1_copies[c], hops[1])
        new = rest_part(1, h1, r0)
        state[pl.ds(r0, chunk), :] = new
        u2[pl.ds(r0, chunk), :] = norm_rows(new)
        send_halo(h2_copies[c], hops[2])
        if c == 0:
            forward_second(2)
    forward_last(2)
    forward_direct(2)
    finish(2)
    for c in range(chunks):
        now_part(2, u2, c * chunk, c * chunk)
    for c in range(chunks):
        r0 = c * chunk
        take_halo(h2_copies[c], hops[2])
        out_ref[pl.ds(r0, chunk), :] = rest_part(2, h2, r0).astype(out_ref.dtype)

    for l in range(layers):
        for m in moves[l]:
            m.wait_send()
    for copy, hop in copies:
        @pl.when(me + hop < n)
        def _(copy=copy):
            copy.wait_send()


def kernel_local(na, nb, sequence_input, w_prev, w_now, conv_bias, w_mix):
    rows, dim = sequence_input.shape
    layers, shard, wide = w_prev.shape
    chunk = rows // 2
    part = DILATIONS[0]
    bf16, f32 = jnp.bfloat16, jnp.float32
    halos = 1 + 2 * (rows // chunk)
    anywhere = pl.BlockSpec(memory_space=pl.ANY)
    vmem = pl.BlockSpec(memory_space=pltpu.VMEM)
    return pl.pallas_call(
        functools.partial(block_kernel, na, nb, chunk),
        out_shape=jax.ShapeDtypeStruct((rows, dim), bf16),
        in_specs=[anywhere, anywhere, anywhere, vmem, anywhere],
        out_specs=vmem,
        scratch_shapes=[
            pltpu.VMEM((layers, na, shard, 2 * wide + dim), bf16),
            pltpu.VMEM((rows, dim), bf16),
            pltpu.VMEM((part, dim), bf16),
            pltpu.VMEM((rows, dim), f32),
            pltpu.VMEM((part + rows, dim), bf16),
            pltpu.VMEM((rows, dim), bf16),
            pltpu.VMEM((rows, dim), bf16),
            pltpu.VMEM((rows, dim), bf16),
            pltpu.VMEM((rows, dim), bf16),
            pltpu.VMEM((rows, wide), f32),
            pltpu.SemaphoreType.DMA((layers, 3)),
            pltpu.SemaphoreType.DMA,
            pltpu.SemaphoreType.DMA((layers, 16)),
            pltpu.SemaphoreType.DMA((layers, 16)),
            pltpu.SemaphoreType.DMA((halos,)),
            pltpu.SemaphoreType.DMA((halos,)),
        ],
        compiler_params=pltpu.CompilerParams(
            collective_id=0, has_side_effects=True, vmem_limit_bytes=56 * 2**20
        ),
    )(sequence_input, w_prev, w_now, conv_bias, jnp.swapaxes(w_mix, 1, 2))


def local(na, nb, sequence_input, w_prev, w_now, conv_bias, w_mix):
    rows = sequence_input.shape[0]
    shard = w_prev.shape[1]
    fits = (
        na == 4
        and nb % GROUP == 0
        and shard % TILE == 0
        and shard > GROUP * 2 * TILE
        and rows % (4 * TILE) == 0
        and DILATIONS[0] < rows
        and DILATIONS[1] % rows == 0
        and DILATIONS[2] % rows == 0
    )
    body = functools.partial(kernel_local, na, nb) if fits else plain_local
    return body(sequence_input, w_prev, w_now, conv_bias, w_mix)


def solution(mesh):
    return jax.shard_map(
        functools.partial(local, mesh.shape["seqa"], mesh.shape["seqb"]),
        mesh=mesh,
        in_specs=(
            P(("seqa", "seqb"), None),
            P(None, "seqa", None),
            P(None, "seqa", None),
            P(),
            P(None, None, "seqa"),
        ),
        out_specs=P(("seqa", "seqb"), None),
        check_vma=False,
    )
```

```python
import functools

import jax
import jax.numpy as jnp
from jax import lax
from jax.experimental import pallas as pl
from jax.experimental.pallas import tpu as pltpu
from jax.sharding import PartitionSpec as P

DILATIONS = (128, 512, 2048)
EPS = 1e-06
TILE = 16
GROUP = 4
MESH_ID = pl.DeviceIdType.MESH


def from_behind(value, axis, by):
    peers = lax.axis_size(axis)
    pairs = [(i, i + by) for i in range(peers) if 0 <= i + by < peers]
    return lax.ppermute(value, axis, pairs)


def norm_rows(values):
    scale = lax.rsqrt(jnp.mean(values * values, axis=1, keepdims=True) + EPS)
    return (values * scale).astype(jnp.bfloat16)


def block_prior(normed, dilation_step):
    rows = normed.shape[0]
    whole = dilation_step // rows
    part = dilation_step % rows
    pieces = []
    if part > 0:
        pieces.append(from_behind(normed[rows - part :], ("seqa", "seqb"), whole + 1))
    head = normed[: rows - part]
    if whole > 0:
        head = from_behind(head, ("seqa", "seqb"), whole)
    pieces.append(head)
    return jnp.concatenate(pieces, axis=0)


def one_layer(hidden_state, tap_prev, tap_now, bias, mixing, dilation_step):
    normed = norm_rows(hidden_state)
    earlier = block_prior(normed, dilation_step)
    dim = hidden_state.shape[1]
    pre = bias[None, :] + jnp.dot(
        earlier,
        lax.all_gather(tap_prev, "seqa", axis=0, tiled=True),
        preferred_element_type=jnp.float32,
    )
    pre = pre + jnp.dot(
        normed,
        lax.all_gather(tap_now, "seqa", axis=0, tiled=True),
        preferred_element_type=jnp.float32,
    )
    hidden = (pre[:, :dim] * jax.nn.sigmoid(pre[:, dim:])).astype(jnp.bfloat16)
    return hidden_state + jnp.dot(
        hidden,
        lax.all_gather(mixing, "seqa", axis=1, tiled=True),
        preferred_element_type=jnp.float32,
    )


def plain_local(sequence_input, w_prev, w_now, conv_bias, w_mix):
    state = sequence_input.astype(jnp.float32)
    for layer, step in enumerate(DILATIONS):
        state = one_layer(
            state, w_prev[layer], w_now[layer], conv_bias[layer], w_mix[layer], step
        )
    return state.astype(jnp.bfloat16)


def flip(value, bit):
    return value + bit - 2 * bit * ((value // bit) % 2)


def block_kernel(
    na, nb, chunk,
    x_hbm, wp_hbm, wn_hbm, bias_ref, wm_hbm,
    out_ref,
    w, xin, xs, state, u0, u1, u2, h1, h2, pre, osend, oin,
    load_sem, x_sem, own_sem, send, recv, halo_send, halo_recv,
):
    layers, dim = wp_hbm.shape[0], x_hbm.shape[1]
    wide = 2 * dim
    shard = wp_hbm.shape[1]
    rows = x_hbm.shape[0]
    n = na * nb
    part = DILATIONS[0]
    a, b = lax.axis_index("seqa"), lax.axis_index("seqb")
    me = a * nb + b
    a1, a2 = flip(a, 1), flip(a, 2)
    b1, b2 = flip(b, 1), flip(b, 2)
    p = b % GROUP
    p1, p2 = flip(p, 1), flip(p, 2)
    p3 = flip(p1, 2)
    big = 2 * TILE
    direct = GROUP * big

    def at(index):
        return (index // nb, index % nb)

    hop = DILATIONS[2] // rows
    half, q = b // hop, b % hop
    other = 1 - half
    pair = (a, (b + hop) % nb)
    follow_a, follow_q = (a + 1) % na, (q + 1) % hop
    wrap = (q + 1) // hop
    next_b = half * hop + follow_q

    loads = []
    for l in range(layers):
        loads.append([
            pltpu.make_async_copy(wp_hbm.at[l], w.at[l, a, :, pl.ds(0, wide)], load_sem.at[l, 0]),
            pltpu.make_async_copy(wn_hbm.at[l], w.at[l, a, :, pl.ds(wide, wide)], load_sem.at[l, 1]),
            pltpu.make_async_copy(wm_hbm.at[l], w.at[l, a, :, pl.ds(2 * wide, dim)], load_sem.at[l, 2]),
        ])
    for c in loads[0]:
        c.start()
    x_load = pltpu.make_async_copy(x_hbm, xin, x_sem)
    x_load.start()
    for l in range(1, layers):
        for c in loads[l]:
            c.start()

    barrier = pltpu.get_barrier_semaphore()
    near = [(a1, b), (a2, b), (a, b1), (a, b2)]
    near += [pair, at((me + 1) % n), at((me + n - 1) % n)]
    near += [at((me + hop - 1) % n), at((me + n - hop + 1) % n)]
    near += [(follow_a, b), ((a + na - 1) % na, b)]
    near += [(a, next_b), (follow_a, next_b)]
    last_b = half * hop + (q + hop - 1) % hop
    near += [(a, last_b), ((a + na - 1) % na, last_b)]
    for dev in near:
        pl.semaphore_signal(barrier, inc=1, device_id=dev, device_id_type=MESH_ID)
    pl.semaphore_wait(barrier, len(near))

    def move(l, k, owner, start, size, dev):
        ref = w.at[l, owner, pl.ds(pl.multiple_of(start, TILE), size)]
        return pltpu.make_async_remote_copy(
            src_ref=ref, dst_ref=ref, send_sem=send.at[l, k], recv_sem=recv.at[l, k],
            device_id=dev, device_id_type=MESH_ID,
        )

    core, across, ynear, znear = (a1, b), (a2, b), (a, b1), (a, b2)
    moves = []
    for l in range(layers):
        moves.append([
            move(l, 0, a, p * big, TILE, across),
            move(l, 1, a, p * big + TILE, TILE, across),
            move(l, 2, a, direct, shard - direct, across),
            move(l, 3, a, 0, shard, core),
            move(l, 4, a2, p * big, TILE, ynear),
            move(l, 5, a2, p * big, TILE, znear),
            move(l, 6, a2, p * big + TILE, TILE, ynear),
            move(l, 7, a2, p * big + TILE, TILE, znear),
            move(l, 8, a2, p * big, big, core),
            move(l, 9, a2, direct, shard - direct, core),
            move(l, 10, a2, p1 * big, TILE, znear),
            move(l, 11, a2, p1 * big, big, core),
            move(l, 12, a2, p2 * big + TILE, TILE, ynear),
            move(l, 13, a2, p2 * big, big, core),
            move(l, 14, a2, p3 * big, TILE, core),
            move(l, 15, a2, p3 * big + TILE, TILE, core),
        ])

    def after(l, k, then):
        moves[l][k].wait_recv()
        for t in then:
            moves[l][t].start()

    def forward_first(l):
        after(l, 0, (4, 5))
        after(l, 1, (6, 7, 8))

    def forward_second(l):
        after(l, 4, (10,))
        after(l, 5, ())
        after(l, 7, (12, 13))
        after(l, 6, (11,))

    def forward_last(l):
        after(l, 10, (14,))
        after(l, 12, (15,))

    def forward_direct(l):
        after(l, 2, (9,))

    def finish(l):
        for k in (3, 8, 9, 11, 13, 14, 15):
            after(l, k, ())

    def halo(src, dst, slot, dev):
        return pltpu.make_async_remote_copy(
            src_ref=src, dst_ref=dst, send_sem=halo_send.at[slot], recv_sem=halo_recv.at[slot],
            device_id=dev, device_id_type=MESH_ID,
        )

    pair_low = halo(xin.at[pl.ds(part, rows - part)], xs.at[0], 0, pair)
    pair_high = halo(xin.at[pl.ds(0, chunk)], xs.at[1, pl.ds(part, chunk)], 0, pair)
    tail_src = xin.at[pl.ds(rows - part, part)]
    tail_next = halo(tail_src, xs.at[0, pl.ds(0, part)], 1, at((me + 1) % n))
    tail_back = halo(tail_src, xs.at[1, pl.ds(0, part)], 2, at((me + n - hop + 1) % n))
    sends_next = jnp.logical_and(me + 1 < n, (b + 1) % nb < hop)
    sends_back = jnp.logical_and(b >= hop - 1, b < 2 * hop - 1)
    takes_next = jnp.logical_and(half == 0, me > 0)

    def second(s):
        to = s + wrap
        slot = to % 2
        dev = ((a + to // 2) % na, next_b)
        return pltpu.make_async_remote_copy(
            src_ref=u1.at[s], dst_ref=h1.at[slot], send_sem=halo_send.at[3 + slot],
            recv_sem=halo_recv.at[3 + slot], device_id=dev, device_id_type=MESH_ID,
        ), a + to // 2 < na

    third = halo(u2.at[1], h2.at[0], 5, (follow_a, b))
    back = halo(osend, oin, 6, pair)

    def send_pair():
        @pl.when(half == 0)
        def _():
            pair_low.start()

        @pl.when(half == 1)
        def _():
            pair_high.start()

    near_cut = (b // 2) % 2 != half
    own_low = pltpu.make_async_copy(xin.at[pl.ds(0, chunk)], xs.at[0, pl.ds(part, chunk)], own_sem)
    own_high = pltpu.make_async_copy(xin.at[pl.ds(part, rows - part)], xs.at[1], own_sem)

    for c in loads[0]:
        c.wait()
    moves[0][0].start()
    moves[0][1].start()
    x_load.wait()

    @pl.when(sends_next)
    def _():
        tail_next.start()

    @pl.when(sends_back)
    def _():
        tail_back.start()

    pl.when(near_cut)(send_pair)

    @pl.when(half == 0)
    def _():
        own_low.start()
        own_low.wait()

    @pl.when(half == 1)
    def _():
        own_high.start()
        own_high.wait()

    for c in loads[1]:
        c.wait()
    moves[1][0].start()
    moves[1][1].start()
    moves[0][2].start()
    moves[0][3].start()
    for c in loads[2]:
        c.wait()
    moves[1][2].start()
    moves[1][3].start()
    for k in (0, 1, 2, 3):
        moves[2][k].start()

    @pl.when(me == 0)
    def _():
        xs[0, pl.ds(0, part), :] = jnp.zeros((part, dim), xs.dtype)

    @pl.when(jnp.logical_and(a == 0, q == 0))
    def _():
        h1[0] = jnp.zeros(h1.shape[1:], h1.dtype)

    @pl.when(a == 0)
    def _():
        h2[0] = jnp.zeros(h2.shape[1:], h2.dtype)

    def enter(s):
        block = xs[s].astype(jnp.float32)
        u0[s] = norm_rows(block)
        state[s] = block[part:]

    forward_first(0)

    @pl.when(takes_next)
    def _():
        tail_next.wait_recv()

    enter(half)
    forward_second(0)
    pl.when(jnp.logical_not(near_cut))(send_pair)
    forward_first(1)
    forward_last(0)
    forward_direct(0)
    finish(0)

    def tap(l, lo):
        return w[l, :, :, lo : lo + wide].reshape(na * shard, wide)

    def now_part(l, now, s):
        pre[s] = bias_ref[l : l + 1, :] + jnp.dot(
            now, tap(l, wide), preferred_element_type=jnp.float32
        )

    def rest_part(l, earlier, s):
        total = pre[s] + jnp.dot(earlier, tap(l, 0), preferred_element_type=jnp.float32)
        hidden = (total[:, :dim] * jax.nn.sigmoid(total[:, dim:])).astype(jnp.bfloat16)
        mix = w[l, :, :, 2 * wide :].reshape(na * shard, dim)
        return state[s] + lax.dot_general(
            hidden, mix, (((1,), (1,)), ((), ())), preferred_element_type=jnp.float32
        )

    for c, s in enumerate((half, other)):
        if c == 1:
            @pl.when(half == 1)
            def _():
                pair_low.wait_recv()

            @pl.when(half == 0)
            def _():
                pair_high.wait_recv()
                tail_back.wait_recv()

            enter(s)
        now_part(0, u0[s, pl.ds(part, chunk), :], s)
        new = rest_part(0, u0[s, pl.ds(0, chunk), :], s)
        state[s] = new
        u1[s] = norm_rows(new)
        copy, there = second(s)
        pl.when(there)(copy.start)
        if c == 0:
            forward_second(1)
    forward_last(1)
    forward_direct(1)
    finish(1)
    for s in (half, other):
        now_part(1, u1[s], s)
    for c, s in enumerate((half, other)):
        @pl.when(jnp.logical_or(me % nb % hop + s > 0, a > 0))
        def _(s=s):
            halo(u1.at[s], h1.at[s], 3 + s, pair).wait_recv()

        new = rest_part(1, h1[s], s)
        state[s] = new
        normed = norm_rows(new)
        u2[s] = normed

        @pl.when(s == 0)
        def _(normed=normed):
            h2[1] = normed

        @pl.when(jnp.logical_and(s == 1, a + 1 < na))
        def _():
            third.start()

        if c == 0:
            forward_first(2)
    forward_second(2)
    forward_last(2)
    forward_direct(2)
    finish(2)
    for c, s in enumerate((other, half)):
        now_part(2, u2[s], s)

        @pl.when(jnp.logical_and(s == 0, a > 0))
        def _():
            third.wait_recv()

        new = rest_part(2, h2[s], s).astype(out_ref.dtype)
        if c == 0:
            osend[...] = new
            back.start()
        else:
            out_ref[pl.ds(pl.multiple_of(half * chunk, chunk), chunk), :] = new
    back.wait_recv()
    out_ref[pl.ds(pl.multiple_of(other * chunk, chunk), chunk), :] = oin[...]

    for l in range(layers):
        for m in moves[l]:
            m.wait_send()
    back.wait_send()
    for s in range(2):
        copy, there = second(s)
        pl.when(there)(copy.wait_send)
    pl.when(a + 1 < na)(third.wait_send)
    pl.when(sends_next)(tail_next.wait_send)
    pl.when(sends_back)(tail_back.wait_send)
    pl.when(half == 0)(pair_low.wait_send)
    pl.when(half == 1)(pair_high.wait_send)


def kernel_local(na, nb, sequence_input, w_prev, w_now, conv_bias, w_mix):
    rows, dim = sequence_input.shape
    layers, shard, wide = w_prev.shape
    chunk = rows // 2
    part = DILATIONS[0]
    bf16, f32 = jnp.bfloat16, jnp.float32
    halos = 7
    anywhere = pl.BlockSpec(memory_space=pl.ANY)
    vmem = pl.BlockSpec(memory_space=pltpu.VMEM)
    return pl.pallas_call(
        functools.partial(block_kernel, na, nb, chunk),
        out_shape=jax.ShapeDtypeStruct((rows, dim), bf16),
        in_specs=[anywhere, anywhere, anywhere, vmem, anywhere],
        out_specs=vmem,
        scratch_shapes=[
            pltpu.VMEM((layers, na, shard, 2 * wide + dim), bf16),
            pltpu.VMEM((rows, dim), bf16),
            pltpu.VMEM((2, part + chunk, dim), bf16),
            pltpu.VMEM((2, chunk, dim), f32),
            pltpu.VMEM((2, part + chunk, dim), bf16),
            pltpu.VMEM((2, chunk, dim), bf16),
            pltpu.VMEM((2, chunk, dim), bf16),
            pltpu.VMEM((2, chunk, dim), bf16),
            pltpu.VMEM((2, chunk, dim), bf16),
            pltpu.VMEM((2, chunk, wide), f32),
            pltpu.VMEM((chunk, dim), bf16),
            pltpu.VMEM((chunk, dim), bf16),
            pltpu.SemaphoreType.DMA((layers, 3)),
            pltpu.SemaphoreType.DMA,
            pltpu.SemaphoreType.DMA,
            pltpu.SemaphoreType.DMA((layers, 16)),
            pltpu.SemaphoreType.DMA((layers, 16)),
            pltpu.SemaphoreType.DMA((halos,)),
            pltpu.SemaphoreType.DMA((halos,)),
        ],
        compiler_params=pltpu.CompilerParams(
            collective_id=0, has_side_effects=True, vmem_limit_bytes=56 * 2**20
        ),
    )(sequence_input, w_prev, w_now, conv_bias, jnp.swapaxes(w_mix, 1, 2))


def local(na, nb, sequence_input, w_prev, w_now, conv_bias, w_mix):
    rows = sequence_input.shape[0]
    shard = w_prev.shape[1]
    fits = (
        na == 4
        and nb % GROUP == 0
        and shard % TILE == 0
        and shard > GROUP * 2 * TILE
        and rows % (4 * TILE) == 0
        and rows == 4 * DILATIONS[0]
        and DILATIONS[1] == rows
        and 2 * DILATIONS[2] == nb * rows
    )
    body = functools.partial(kernel_local, na, nb) if fits else plain_local
    return body(sequence_input, w_prev, w_now, conv_bias, w_mix)


def solution(mesh):
    return jax.shard_map(
        functools.partial(local, mesh.shape["seqa"], mesh.shape["seqb"]),
        mesh=mesh,
        in_specs=(
            P(("seqa", "seqb"), None),
            P(None, "seqa", None),
            P(None, "seqa", None),
            P(),
            P(None, None, "seqa"),
        ),
        out_specs=P(("seqa", "seqb"), None),
        check_vma=False,
    )
```

```python
import functools

import jax
import jax.numpy as jnp
from jax import lax
from jax.experimental import pallas as pl
from jax.experimental.pallas import tpu as pltpu
from jax.sharding import PartitionSpec as P

DILATIONS = (128, 512, 2048)
EPS = 1e-06
TILE = 16
GROUP = 4
MESH_ID = pl.DeviceIdType.MESH


def from_behind(value, axis, by):
    peers = lax.axis_size(axis)
    pairs = [(i, i + by) for i in range(peers) if 0 <= i + by < peers]
    return lax.ppermute(value, axis, pairs)


def norm_rows(values):
    scale = lax.rsqrt(jnp.mean(values * values, axis=1, keepdims=True) + EPS)
    return (values * scale).astype(jnp.bfloat16)


def block_prior(normed, dilation_step):
    rows = normed.shape[0]
    whole = dilation_step // rows
    part = dilation_step % rows
    pieces = []
    if part > 0:
        pieces.append(from_behind(normed[rows - part :], ("seqa", "seqb"), whole + 1))
    head = normed[: rows - part]
    if whole > 0:
        head = from_behind(head, ("seqa", "seqb"), whole)
    pieces.append(head)
    return jnp.concatenate(pieces, axis=0)


def one_layer(hidden_state, tap_prev, tap_now, bias, mixing, dilation_step):
    normed = norm_rows(hidden_state)
    earlier = block_prior(normed, dilation_step)
    dim = hidden_state.shape[1]
    pre = bias[None, :] + jnp.dot(
        earlier,
        lax.all_gather(tap_prev, "seqa", axis=0, tiled=True),
        preferred_element_type=jnp.float32,
    )
    pre = pre + jnp.dot(
        normed,
        lax.all_gather(tap_now, "seqa", axis=0, tiled=True),
        preferred_element_type=jnp.float32,
    )
    hidden = (pre[:, :dim] * jax.nn.sigmoid(pre[:, dim:])).astype(jnp.bfloat16)
    return hidden_state + jnp.dot(
        hidden,
        lax.all_gather(mixing, "seqa", axis=1, tiled=True),
        preferred_element_type=jnp.float32,
    )


def plain_local(sequence_input, w_prev, w_now, conv_bias, w_mix):
    state = sequence_input.astype(jnp.float32)
    for layer, step in enumerate(DILATIONS):
        state = one_layer(
            state, w_prev[layer], w_now[layer], conv_bias[layer], w_mix[layer], step
        )
    return state.astype(jnp.bfloat16)


def flip(value, bit):
    return value + bit - 2 * bit * ((value // bit) % 2)


def block_kernel(
    na, nb, chunk,
    x_hbm, wp_hbm, wn_hbm, bias_ref, wm_hbm,
    out_ref,
    w, xin, xs, state, u0, u1, u2, h1, h2, pre, osend, oin,
    load_sem, x_sem, own_sem, send, recv, halo_send, halo_recv,
):
    layers, dim = wp_hbm.shape[0], x_hbm.shape[1]
    wide = 2 * dim
    shard = wp_hbm.shape[1]
    rows = x_hbm.shape[0]
    n = na * nb
    part = DILATIONS[0]
    a, b = lax.axis_index("seqa"), lax.axis_index("seqb")
    me = a * nb + b
    a1, a2 = flip(a, 1), flip(a, 2)
    b1, b2 = flip(b, 1), flip(b, 2)
    p = b % GROUP
    p1, p2 = flip(p, 1), flip(p, 2)
    p3 = flip(p1, 2)
    big = 2 * TILE
    direct = GROUP * big

    def at(index):
        return (index // nb, index % nb)

    hop = DILATIONS[2] // rows
    half, q = b // hop, b % hop
    other = 1 - half
    pair = (a, (b + hop) % nb)
    follow_a, follow_q = (a + 1) % na, (q + 1) % hop
    wrap = (q + 1) // hop
    next_b = half * hop + follow_q

    loads = []
    for l in range(layers):
        loads.append([
            pltpu.make_async_copy(wp_hbm.at[l], w.at[l, a, :, pl.ds(0, wide)], load_sem.at[l, 0]),
            pltpu.make_async_copy(wn_hbm.at[l], w.at[l, a, :, pl.ds(wide, wide)], load_sem.at[l, 1]),
            pltpu.make_async_copy(wm_hbm.at[l], w.at[l, a, :, pl.ds(2 * wide, dim)], load_sem.at[l, 2]),
        ])
    for c in loads[0]:
        c.start()
    x_load = pltpu.make_async_copy(x_hbm, xin, x_sem)
    x_load.start()
    barrier = pltpu.get_barrier_semaphore()
    near = [(a1, b), (a2, b), (a, b1), (a, b2)]
    near += [pair, at((me + 1) % n), at((me + n - 1) % n)]
    near += [at((me + hop - 1) % n), at((me + n - hop + 1) % n)]
    near += [(follow_a, b), ((a + na - 1) % na, b)]
    near += [(a, next_b), (follow_a, next_b)]
    last_b = half * hop + (q + hop - 1) % hop
    near += [(a, last_b), ((a + na - 1) % na, last_b)]
    for dev in near:
        pl.semaphore_signal(barrier, inc=1, device_id=dev, device_id_type=MESH_ID)
    pl.semaphore_wait(barrier, len(near))

    def move(l, k, owner, start, size, dev):
        ref = w.at[l, owner, pl.ds(pl.multiple_of(start, TILE), size)]
        return pltpu.make_async_remote_copy(
            src_ref=ref, dst_ref=ref, send_sem=send.at[l, k], recv_sem=recv.at[l, k],
            device_id=dev, device_id_type=MESH_ID,
        )

    core, across, ynear, znear = (a1, b), (a2, b), (a, b1), (a, b2)
    moves = []
    for l in range(layers):
        moves.append([
            move(l, 0, a, p * big, TILE, across),
            move(l, 1, a, p * big + TILE, TILE, across),
            move(l, 2, a, direct, shard - direct, across),
            move(l, 3, a, 0, shard, core),
            move(l, 4, a2, p * big, TILE, ynear),
            move(l, 5, a2, p * big, TILE, znear),
            move(l, 6, a2, p * big + TILE, TILE, ynear),
            move(l, 7, a2, p * big + TILE, TILE, znear),
            move(l, 8, a2, p * big, big, core),
            move(l, 9, a2, direct, shard - direct, core),
            move(l, 10, a2, p1 * big, TILE, znear),
            move(l, 11, a2, p1 * big, big, core),
            move(l, 12, a2, p2 * big + TILE, TILE, ynear),
            move(l, 13, a2, p2 * big, big, core),
            move(l, 14, a2, p3 * big, TILE, core),
            move(l, 15, a2, p3 * big + TILE, TILE, core),
        ])

    def after(l, k, then):
        moves[l][k].wait_recv()
        for t in then:
            moves[l][t].start()

    def forward_first(l):
        after(l, 0, (4, 5))
        after(l, 1, (6, 7, 8))

    def forward_second(l):
        after(l, 4, (10,))
        after(l, 5, ())
        after(l, 7, (12, 13))
        after(l, 6, (11,))

    def forward_last(l):
        after(l, 10, (14,))
        after(l, 12, (15,))

    def forward_direct(l):
        after(l, 2, (9,))

    def finish(l):
        for k in (3, 8, 9, 11, 13, 14, 15):
            after(l, k, ())

    def halo(src, dst, slot, dev):
        return pltpu.make_async_remote_copy(
            src_ref=src, dst_ref=dst, send_sem=halo_send.at[slot], recv_sem=halo_recv.at[slot],
            device_id=dev, device_id_type=MESH_ID,
        )

    pair_low = halo(xin.at[pl.ds(part, rows - part)], xs.at[0], 0, pair)
    pair_high = halo(xin.at[pl.ds(0, chunk)], xs.at[1, pl.ds(part, chunk)], 0, pair)
    tail_src = xin.at[pl.ds(rows - part, part)]
    tail_next = halo(tail_src, xs.at[0, pl.ds(0, part)], 1, at((me + 1) % n))
    tail_back = halo(tail_src, xs.at[1, pl.ds(0, part)], 2, at((me + n - hop + 1) % n))
    sends_next = jnp.logical_and(me + 1 < n, (b + 1) % nb < hop)
    sends_back = jnp.logical_and(b >= hop - 1, b < 2 * hop - 1)
    takes_next = jnp.logical_and(half == 0, me > 0)

    def second(s):
        to = s + wrap
        slot = to % 2
        dev = ((a + to // 2) % na, next_b)
        return pltpu.make_async_remote_copy(
            src_ref=u1.at[s], dst_ref=h1.at[slot], send_sem=halo_send.at[3 + slot],
            recv_sem=halo_recv.at[3 + slot], device_id=dev, device_id_type=MESH_ID,
        ), a + to // 2 < na

    third = halo(u2.at[1], h2.at[0], 5, (follow_a, b))
    back = halo(osend, oin, 6, pair)

    def send_pair():
        @pl.when(half == 0)
        def _():
            pair_low.start()

        @pl.when(half == 1)
        def _():
            pair_high.start()

    near_cut = (b // 2) % 2 != half
    own_low = pltpu.make_async_copy(xin.at[pl.ds(0, chunk)], xs.at[0, pl.ds(part, chunk)], own_sem)
    own_high = pltpu.make_async_copy(xin.at[pl.ds(part, rows - part)], xs.at[1], own_sem)

    for c in loads[0]:
        c.wait()
    moves[0][0].start()
    moves[0][1].start()
    for c in loads[1]:
        c.start()
    x_load.wait()

    @pl.when(sends_next)
    def _():
        tail_next.start()

    @pl.when(sends_back)
    def _():
        tail_back.start()

    pl.when(near_cut)(send_pair)

    @pl.when(half == 0)
    def _():
        own_low.start()
        own_low.wait()

    @pl.when(half == 1)
    def _():
        own_high.start()
        own_high.wait()

    for c in loads[1]:
        c.wait()
    for c in loads[2]:
        c.start()
    moves[1][0].start()
    moves[1][1].start()
    moves[0][2].start()
    moves[0][3].start()
    for c in loads[2]:
        c.wait()
    moves[1][2].start()
    moves[1][3].start()
    for k in (0, 1, 2, 3):
        moves[2][k].start()

    @pl.when(me == 0)
    def _():
        xs[0, pl.ds(0, part), :] = jnp.zeros((part, dim), xs.dtype)

    @pl.when(jnp.logical_and(a == 0, q == 0))
    def _():
        h1[0] = jnp.zeros(h1.shape[1:], h1.dtype)

    @pl.when(a == 0)
    def _():
        h2[0] = jnp.zeros(h2.shape[1:], h2.dtype)

    def enter(s):
        block = xs[s].astype(jnp.float32)
        u0[s] = norm_rows(block)
        state[s] = block[part:]

    forward_first(0)

    @pl.when(takes_next)
    def _():
        tail_next.wait_recv()

    enter(half)
    forward_second(0)
    pl.when(jnp.logical_not(near_cut))(send_pair)
    forward_first(1)
    forward_last(0)
    forward_direct(0)
    finish(0)

    def tap(l, lo):
        return w[l, :, :, lo : lo + wide].reshape(na * shard, wide)

    def now_part(l, now, s):
        pre[s] = bias_ref[l : l + 1, :] + jnp.dot(
            now, tap(l, wide), preferred_element_type=jnp.float32
        )

    def rest_part(l, earlier, s):
        total = pre[s] + jnp.dot(earlier, tap(l, 0), preferred_element_type=jnp.float32)
        hidden = (total[:, :dim] * jax.nn.sigmoid(total[:, dim:])).astype(jnp.bfloat16)
        mix = w[l, :, :, 2 * wide :].reshape(na * shard, dim)
        return state[s] + lax.dot_general(
            hidden, mix, (((1,), (1,)), ((), ())), preferred_element_type=jnp.float32
        )

    for c, s in enumerate((half, other)):
        if c == 1:
            @pl.when(half == 1)
            def _():
                pair_low.wait_recv()

            @pl.when(half == 0)
            def _():
                pair_high.wait_recv()
                tail_back.wait_recv()

            enter(s)
        now_part(0, u0[s, pl.ds(part, chunk), :], s)
        if c == 1:
            forward_first(2)
        new = rest_part(0, u0[s, pl.ds(0, chunk), :], s)
        state[s] = new
        u1[s] = norm_rows(new)
        copy, there = second(s)
        pl.when(there)(copy.start)
        if c == 0:
            forward_second(1)
    forward_last(1)
    forward_direct(1)
    finish(1)
    for s in (half, other):
        now_part(1, u1[s], s)
    forward_second(2)
    for c, s in enumerate((half, other)):
        @pl.when(jnp.logical_or(me % nb % hop + s > 0, a > 0))
        def _(s=s):
            halo(u1.at[s], h1.at[s], 3 + s, pair).wait_recv()

        new = rest_part(1, h1[s], s)
        state[s] = new
        normed = norm_rows(new)
        u2[s] = normed

        @pl.when(s == 0)
        def _(normed=normed):
            h2[1] = normed

        @pl.when(jnp.logical_and(s == 1, a + 1 < na))
        def _():
            third.start()

    forward_last(2)
    forward_direct(2)
    finish(2)
    for c, s in enumerate((other, half)):
        now_part(2, u2[s], s)

        @pl.when(jnp.logical_and(s == 0, a > 0))
        def _():
            third.wait_recv()

        new = rest_part(2, h2[s], s).astype(out_ref.dtype)
        if c == 0:
            osend[...] = new
            back.start()
        else:
            out_ref[pl.ds(pl.multiple_of(half * chunk, chunk), chunk), :] = new
    back.wait_recv()
    out_ref[pl.ds(pl.multiple_of(other * chunk, chunk), chunk), :] = oin[...]

    for l in range(layers):
        for m in moves[l]:
            m.wait_send()
    back.wait_send()
    for s in range(2):
        copy, there = second(s)
        pl.when(there)(copy.wait_send)
    pl.when(a + 1 < na)(third.wait_send)
    pl.when(sends_next)(tail_next.wait_send)
    pl.when(sends_back)(tail_back.wait_send)
    pl.when(half == 0)(pair_low.wait_send)
    pl.when(half == 1)(pair_high.wait_send)


def kernel_local(na, nb, sequence_input, w_prev, w_now, conv_bias, w_mix):
    rows, dim = sequence_input.shape
    layers, shard, wide = w_prev.shape
    chunk = rows // 2
    part = DILATIONS[0]
    bf16, f32 = jnp.bfloat16, jnp.float32
    halos = 7
    anywhere = pl.BlockSpec(memory_space=pl.ANY)
    vmem = pl.BlockSpec(memory_space=pltpu.VMEM)
    return pl.pallas_call(
        functools.partial(block_kernel, na, nb, chunk),
        out_shape=jax.ShapeDtypeStruct((rows, dim), bf16),
        in_specs=[anywhere, anywhere, anywhere, vmem, anywhere],
        out_specs=vmem,
        scratch_shapes=[
            pltpu.VMEM((layers, na, shard, 2 * wide + dim), bf16),
            pltpu.VMEM((rows, dim), bf16),
            pltpu.VMEM((2, part + chunk, dim), bf16),
            pltpu.VMEM((2, chunk, dim), f32),
            pltpu.VMEM((2, part + chunk, dim), bf16),
            pltpu.VMEM((2, chunk, dim), bf16),
            pltpu.VMEM((2, chunk, dim), bf16),
            pltpu.VMEM((2, chunk, dim), bf16),
            pltpu.VMEM((2, chunk, dim), bf16),
            pltpu.VMEM((2, chunk, wide), f32),
            pltpu.VMEM((chunk, dim), bf16),
            pltpu.VMEM((chunk, dim), bf16),
            pltpu.SemaphoreType.DMA((layers, 3)),
            pltpu.SemaphoreType.DMA,
            pltpu.SemaphoreType.DMA,
            pltpu.SemaphoreType.DMA((layers, 16)),
            pltpu.SemaphoreType.DMA((layers, 16)),
            pltpu.SemaphoreType.DMA((halos,)),
            pltpu.SemaphoreType.DMA((halos,)),
        ],
        compiler_params=pltpu.CompilerParams(
            collective_id=0, has_side_effects=True, vmem_limit_bytes=56 * 2**20
        ),
    )(sequence_input, w_prev, w_now, conv_bias, jnp.swapaxes(w_mix, 1, 2))


def local(na, nb, sequence_input, w_prev, w_now, conv_bias, w_mix):
    rows = sequence_input.shape[0]
    shard = w_prev.shape[1]
    fits = (
        na == 4
        and nb % GROUP == 0
        and shard % TILE == 0
        and shard > GROUP * 2 * TILE
        and rows % (4 * TILE) == 0
        and rows == 4 * DILATIONS[0]
        and DILATIONS[1] == rows
        and 2 * DILATIONS[2] == nb * rows
    )
    body = functools.partial(kernel_local, na, nb) if fits else plain_local
    return body(sequence_input, w_prev, w_now, conv_bias, w_mix)


def solution(mesh):
    return jax.shard_map(
        functools.partial(local, mesh.shape["seqa"], mesh.shape["seqb"]),
        mesh=mesh,
        in_specs=(
            P(("seqa", "seqb"), None),
            P(None, "seqa", None),
            P(None, "seqa", None),
            P(),
            P(None, None, "seqa"),
        ),
        out_specs=P(("seqa", "seqb"), None),
        check_vma=False,
    )
```
